256 devices in a mesh: blk: 32 (over y_hi, z, core), rep: 8 (over x, y_lo).
Axes of the slice: x: 4, y: 4 (y_hi: 2, y_lo: 2; y = y_hi * 2 + y_lo), z: 8, core: 2. Of those that a mesh axis runs over, the one named last changes fastest.
Arguments:
- features: float32 [32768, 128], P('blk'), may hold values from -6 to 6
- factors: float32 [32768, 128], P('blk'), may hold values from -2.4 to 2.4
Outputs:
- grads: float32 [32768, 128], P(('blk', 'rep'))
The draws below stay inside these ranges and needn't reach their ends.
All inputs are finite; a program needn't handle non-finite values.
Results may differ from the reference program's by a relative error of at most 0.00018.
Values sent between devices are 32-bit elements; how exact they have to be, the bound alone decides.
A program may use at most 128 MiB of HBM per device.

```python
import jax
import jax.numpy as jnp
from jax import lax

D = 128
RANK = 64
P_DEV = 1024
POINTS = 32768
N_BLK = 32


def level_of(key, extent, cuts, low, high):
    level = 1.0
    for position, shards_of in cuts:
        draws = jax.random.uniform(jax.random.fold_in(jax.random.fold_in(key, 6), position), (shards_of,), jnp.float32, low / len(cuts), high / len(cuts))
        level = level * jnp.repeat(jnp.exp(draws), extent[position] // shards_of).reshape((-1,) + (1,) * (len(extent) - 1 - position))
    return level


def noise(stream_key, extent, spread, limit, cuts=(), dtype=jnp.bfloat16):
    entries = jax.random.normal(stream_key, extent, jnp.float32) * spread
    if len(cuts) > 0:
        entries = level_of(stream_key, extent, cuts, -0.22, 0.18) * entries
    return jnp.clip(entries, min=-limit, max=limit).astype(dtype)


def setup_inputs(seed: int = 0) -> dict:
    seeds = jax.random.split(jax.random.key(seed), 3)
    features = noise(seeds[0], (POINTS, D), 1.0, 6.0, ((0, 32),), jnp.float32)
    factors = noise(seeds[1], (POINTS, 2 * RANK), 0.4, 2.4, ((0, 32),), jnp.float32)
    return {"features": features, "factors": factors}


def reference(features, factors):
    hi = lax.Precision.HIGHEST
    width = features.shape[1]
    all_sq = lax.optimization_barrier(jnp.sum(features * features, axis=1))
    rows_f = features.reshape(N_BLK, P_DEV, width)
    rows_c = factors.reshape(N_BLK, P_DEV, 2 * RANK)

    def block_grad(pair):
        own_feat, own_fac = pair
        cross = jnp.dot(own_feat, features.T, precision=hi)
        own_sq = lax.optimization_barrier(jnp.sum(own_feat * own_feat, axis=1))
        sq_dist = own_sq[:, None] + all_sq[None, :] - 2.0 * cross
        kernel = jnp.exp(-sq_dist / (2.0 * width))
        coupling = jnp.dot(own_fac[:, :RANK], factors[:, RANK:].T, precision=hi)
        coupling = coupling + jnp.dot(own_fac[:, RANK:], factors[:, :RANK].T, precision=hi)
        weight = coupling * kernel
        total = lax.optimization_barrier(jnp.sum(weight, axis=1))[:, None] * own_feat - jnp.dot(weight, features, precision=hi)
        return -total / width
    out = lax.map(block_grad, (rows_f, rows_c))
    return out.reshape(N_BLK * P_DEV, width)
```

```python
import functools
import math

import jax
import jax.numpy as jnp
from jax import lax
from jax.experimental import pallas as pl
from jax.experimental.pallas import tpu as pltpu
from jax.sharding import PartitionSpec as P

MESH = pl.DeviceIdType.MESH
F32, BF16 = jnp.float32, jnp.bfloat16

NAMES = ["s0", "s1", "s-1", "o0", "s2", "s-2", "o1", "s3", "s-3", "o2", "s4", "o-2", "o-1", "o3", "o-3", "o4"]
SLOT = {name: i for i, name in enumerate(NAMES)}
GROUPS = [["s0"], NAMES[1:4], NAMES[4:7], NAMES[7:10], NAMES[10:13], NAMES[13:16]]


def split(v):
    hi = v.astype(BF16)
    lo = (v - hi.astype(F32)).astype(BF16)
    return hi, lo


def kernel(count, share, width, feat, fac, out, part, x, g, y, h, f, acc, sums, stage, landed,
           recv, sent, sib_sent, local, red_sent, red_recv):
    rank = width // 2
    scale = math.log2(math.e) / (2.0 * width)
    blk, rep = lax.axis_index("blk"), lax.axis_index("rep")
    core, zpos, y_hi = blk % 2, (blk // 2) % 8, blk // 16
    y_lo = rep % 2
    down = {"blk": y_hi * 16 + (zpos + 7) % 8 * 2 + core, "rep": rep}
    up = {"blk": y_hi * 16 + (zpos + 1) % 8 * 2 + core, "rep": rep}
    side = {"blk": (1 - y_hi) * 16 + zpos * 2 + core, "rep": rep + 1 - 2 * y_lo}
    sibling = {"blk": blk + 1 - 2 * core, "rep": rep}
    pick = rep // 2 * 2 + (y_lo + y_hi) % 2
    rows = pl.ds(pl.multiple_of(pick * share, share), share)

    barrier = pltpu.get_barrier_semaphore()
    for peer in (down, up, side, sibling):
        pl.semaphore_signal(barrier, inc=1, device_id=peer, device_id_type=MESH)
    for k in range(1, 8):
        pl.semaphore_signal(barrier, inc=1, device_id={"blk": blk, "rep": (rep + k) % 8}, device_id_type=MESH)
    pl.semaphore_wait(barrier, 11)

    pending = []

    def send(name, fc, to, dst, stream=0):
        source = part.at[SLOT[name], 0, fc] if name != "s0" else (feat, fac)[fc].at[rows, :]
        sems = sent if stream == 0 else sib_sent
        copy = pltpu.make_async_remote_copy(
            src_ref=source,
            dst_ref=part.at[SLOT[dst], stream, fc],
            send_sem=sems.at[SLOT[dst], fc],
            recv_sem=recv.at[SLOT[dst], stream, fc],
            device_id=to,
            device_id_type=MESH,
        )
        copy.start()
        pending.append(copy)

    def arrive(name, fc, stream=0):
        buf = part.at[SLOT[name], stream, fc]
        sems = sent if stream == 0 else sib_sent
        pltpu.make_async_remote_copy(
            src_ref=buf, dst_ref=buf, send_sem=sems.at[SLOT[name], fc], recv_sem=recv.at[SLOT[name], stream, fc],
            device_id=sibling, device_id_type=MESH,
        ).wait_recv()

    def relay(name, fc, *onward):
        arrive(name, fc)
        for to, dst in onward:
            send(name, fc, to, dst)
        send(name, fc, sibling, name, 1)

    for fc in (0, 1):
        send("s0", fc, down, "s1")
        send("s0", fc, up, "s-1")
        send("s0", fc, side, "o0")
        send("s0", fc, sibling, "s0", 1)
    own = [
        pltpu.make_async_copy((feat, fac)[fc].at[rows, :], part.at[0, 0, fc], local.at[fc]) for fc in (0, 1)
    ]
    for copy in own:
        copy.start()

    fo = feat[...]
    norm = jnp.exp2(-scale * jnp.sum(fo * fo, axis=1, keepdims=True))
    for ref, value in ((x, fo * (2.0 * scale)), (g, fac[...] * norm)):
        hi, lo = split(value)
        for k, piece in enumerate((hi, lo, hi, lo)):
            ref[:, k * width:(k + 1) * width] = piece
    acc[...] = jnp.zeros_like(acc)
    sums[...] = jnp.zeros_like(sums)

    def prepare(names):
        for k, name in enumerate(names):
            cols = slice(k * 2 * share, (k + 1) * 2 * share)
            pf = part[SLOT[name], :, 0].reshape(2 * share, width)
            pc = part[SLOT[name], :, 1].reshape(2 * share, width)
            hi, lo = split(pf)
            f[cols, 0:width] = hi
            f[cols, width:2 * width] = lo
            hi, lo = hi.T, lo.T
            for n, piece in enumerate((hi, hi, lo, lo)):
                y[n * width:(n + 1) * width, cols] = piece
            norm = jnp.exp2(-scale * jnp.sum(pf * pf, axis=1, keepdims=True))
            hi, lo = split(pc * norm)
            hi, lo = hi.T, lo.T
            hi = jnp.concatenate([hi[rank:], hi[:rank]], axis=0)
            lo = jnp.concatenate([lo[rank:], lo[:rank]], axis=0)
            for n, piece in enumerate((hi, hi, lo, lo)):
                h[n * width:(n + 1) * width, cols] = piece

    def unit(r, points, band=256):
        mine = pl.ds(pl.multiple_of(r * band, band), band)
        s = jnp.dot(x[mine, :], y[:, :points], preferred_element_type=F32)
        c = jnp.dot(g[mine, :], h[:, :points], preferred_element_type=F32)
        w = c * jnp.exp2(s)
        total = w[:, :width]
        for k in range(1, points // width):
            total = total + w[:, k * width:(k + 1) * width]
        sums[mine, :] += total
        hi, lo = split(w)
        acc[mine, :] += jnp.dot(hi, f[:points, :], preferred_element_type=F32) + jnp.dot(
            lo, f[:points, :], preferred_element_type=F32
        )

    def bands(first, last, points):
        lax.fori_loop(first, last, lambda r, c: (unit(r, points), c)[1], 0)

    def ready(names):
        for name in names:
            for fc in (0, 1):
                arrive(name, fc, 1)
        prepare(names)

    def first_hop(fc):
        relay("s1", fc, (down, "s2"), (side, "o1"))
        relay("s-1", fc, (up, "s-2"))
        relay("o0", fc)

    def second_hop(fc):
        relay("s2", fc, (down, "s3"), (side, "o2"))
        relay("s-2", fc, (up, "s-3"))
        relay("o1", fc)

    def third_hop(fc):
        relay("s3", fc, *(((down, "s4"),) if fc == 0 else ()))
        relay("s-3", fc, *(((up, "s4"),) if fc == 1 else ()))
        relay("o2", fc, (down, "o3"))
        send("s-2", fc, side, "o-2")
        send("s-1", fc, side, "o-1")

    for copy in own:
        copy.wait()
    ready(GROUPS[0])
    bands(0, 4, 256)
    first_hop(0)
    first_hop(1)
    ready(GROUPS[1])
    bands(0, 2, 768)
    second_hop(0)
    bands(2, 4, 768)
    second_hop(1)
    ready(GROUPS[2])
    bands(0, 2, 768)
    third_hop(0)
    bands(2, 4, 768)
    third_hop(1)
    ready(GROUPS[3])
    bands(0, 2, 768)
    relay("s4", 0)
    relay("s4", 1)
    relay("o-2", 0, (up, "o-3"))
    relay("o3", 0, (down, "o4"))
    bands(2, 4, 768)
    relay("o-2", 1, (up, "o-3"))
    relay("o3", 1, (down, "o4"))
    relay("o-1", 0)
    relay("o-1", 1)
    ready(GROUPS[4])
    bands(0, 2, 768)
    relay("o-3", 0)
    relay("o4", 0)
    bands(2, 4, 768)
    relay("o-3", 1)
    relay("o4", 1)
    ready(GROUPS[5])

    def reduce_copy(k):
        return pltpu.make_async_remote_copy(
            src_ref=stage.at[k], dst_ref=landed.at[k], send_sem=red_sent.at[k], recv_sem=red_recv.at[k],
            device_id={"blk": blk, "rep": (rep // 2 + 1 + k // 2) % 4 * 2 + (y_lo + 1 + k) % 2}, device_id_type=MESH,
        )

    def finish(n, c):
        r = (rep // 2 + 1 + n) % 4
        unit(r, 768)
        for k in (0, 1):
            lane = pl.ds(pl.multiple_of((r * 2 + (y_lo + 1 + k) % 2) * share, share), share)
            row_sum = jnp.sum(sums[lane, :], axis=1, keepdims=True)
            total = row_sum * feat[lane, :] - (acc[lane, :width] + acc[lane, width:])
            stage[2 * n + k] = total * (-1.0 / width)
        return c

    for n in range(4):
        finish(n, 0)
        for k in (0, 1):
            if 2 * n + k < 7:
                reduce_copy(2 * n + k).start()
    for k in range(7):
        reduce_copy(k).wait_recv()
    total = stage[7]
    for k in range(7):
        total = total + landed[k]
    out[...] = total
    for copy in pending:
        copy.wait_send()
    for k in range(7):
        reduce_copy(k).wait_send()


def solution(mesh):
    def body(features, factors):
        count, width = features.shape
        share = count // 8
        dma = pltpu.SemaphoreType.DMA
        vmem = pltpu.VMEM
        return pl.pallas_call(
            functools.partial(kernel, count, share, width),
            out_shape=jax.ShapeDtypeStruct((share, width), F32),
            in_specs=[pl.BlockSpec(memory_space=vmem)] * 2,
            out_specs=pl.BlockSpec(memory_space=vmem),
            scratch_shapes=[
                vmem((16, 2, 2, share, width), F32),
                vmem((count, 4 * width), BF16),
                vmem((count, 4 * width), BF16),
                vmem((4 * width, 768), BF16),
                vmem((4 * width, 768), BF16),
                vmem((768, 2 * width), BF16),
                vmem((count, 2 * width), F32),
                vmem((count, width), F32),
                vmem((8, share, width), F32),
                vmem((7, share, width), F32),
                dma((16, 2, 2)),
                dma((16, 2)),
                dma((16, 2)),
                dma((2,)),
                dma((7,)),
                dma((7,)),
            ],
            compiler_params=pltpu.CompilerParams(
                collective_id=0, has_side_effects=True, vmem_limit_bytes=56 * 1024 * 1024
            ),
            name="grads",
        )(features, factors)

    placed = (P("blk", None), P("blk", None))
    return jax.shard_map(
        body, mesh=mesh, in_specs=placed, out_specs=P(("blk", "rep"), None), check_vma=False
    )
```

```python
import functools
import math

import jax
import jax.numpy as jnp
from jax import lax
from jax.experimental import pallas as pl
from jax.experimental.pallas import tpu as pltpu
from jax.sharding import PartitionSpec as P

MESH = pl.DeviceIdType.MESH
F32, BF16 = jnp.float32, jnp.bfloat16

NAMES = ["s0", "s1", "s-1", "o0", "s2", "s-2", "o1", "s3", "s-3", "o2", "o3", "s4", "o-2", "o4", "o-3", "o-1"]
SLOT = {name: i for i, name in enumerate(NAMES)}
SOURCES = [("s0", "s0", "s0"), ("s1", "s-1", "s1"), ("s2", "s-2", "s2"), ("o2", "s-3", "s-2"), ("o3", "o-2", "s-1")]


def split(v):
    hi = v.astype(BF16)
    lo = (v - hi.astype(F32)).astype(BF16)
    return hi, lo


def kernel(count, share, width, feat, fac, out, part, x, g, y, h, f, acc, sums, stage, landed,
           recv, sib_recv, sent, sib_sent, local, red_sent, red_recv):
    rank = width // 2
    scale = math.log2(math.e) / (2.0 * width)
    blk, rep = lax.axis_index("blk"), lax.axis_index("rep")
    core, zpos, y_hi = blk % 2, (blk // 2) % 8, blk // 16
    y_lo = rep % 2
    down = {"blk": y_hi * 16 + (zpos + 7) % 8 * 2 + core, "rep": rep}
    up = {"blk": y_hi * 16 + (zpos + 1) % 8 * 2 + core, "rep": rep}
    side = {"blk": (1 - y_hi) * 16 + zpos * 2 + core, "rep": rep + 1 - 2 * y_lo}
    sibling = {"blk": blk + 1 - 2 * core, "rep": rep}
    pick = rep // 2 * 2 + (y_lo + y_hi) % 2
    rows = pl.ds(pl.multiple_of(pick * share, share), share)

    barrier = pltpu.get_barrier_semaphore()
    for peer in (down, up, side, sibling):
        pl.semaphore_signal(barrier, inc=1, device_id=peer, device_id_type=MESH)
    for k in range(1, 8):
        pl.semaphore_signal(barrier, inc=1, device_id={"blk": blk, "rep": (rep + k) % 8}, device_id_type=MESH)
    pl.semaphore_wait(barrier, 11)

    def remote(src, dst, send_sem, recv_sem, to):
        return pltpu.make_async_remote_copy(
            src_ref=src, dst_ref=dst, send_sem=send_sem, recv_sem=recv_sem, device_id=to, device_id_type=MESH
        )

    def send_round(k, fc):
        for n, (name, to) in enumerate(zip(SOURCES[k - 1], (down, up, side))):
            source = part.at[0, fc, SLOT[name]] if name != "s0" else (feat, fac)[fc].at[rows, :]
            remote(source, part.at[0, fc, 3 * k - 2 + n], sent, recv.at[k, fc], to).start()

    def of_round(stream, k, fc):
        return part.at[stream, fc, pl.ds(3 * k - 2, 3)]

    def take_round(k, fc):
        mine, theirs = of_round(0, k, fc), of_round(1, k, fc)
        remote(mine, mine, sent, recv.at[k, fc], sibling).wait_recv()
        if k < 5:
            send_round(k + 1, fc)
        remote(mine, theirs, sib_sent, sib_recv.at[k, fc], sibling).start()

    def take_sibling(k):
        for fc in (0, 1):
            buf = of_round(1, k, fc) if k else part.at[1, fc, 0]
            remote(buf, buf, sib_sent, sib_recv.at[k, fc], sibling).wait_recv()

    for fc in (0, 1):
        send_round(1, fc)
    for fc in (0, 1):
        remote((feat, fac)[fc].at[rows, :], part.at[1, fc, 0], sib_sent, sib_recv.at[0, fc], sibling).start()
    own = [
        pltpu.make_async_copy((feat, fac)[fc].at[rows, :], part.at[0, fc, 0], local.at[fc]) for fc in (0, 1)
    ]
    for copy in own:
        copy.start()

    fo = feat[...]
    norm = jnp.exp2(-scale * jnp.sum(fo * fo, axis=1, keepdims=True))
    for ref, value in ((x, fo * (2.0 * scale)), (g, fac[...] * norm)):
        hi, lo = split(value)
        for k, piece in enumerate((hi, lo, hi, lo)):
            ref[:, k * width:(k + 1) * width] = piece
    acc[...] = jnp.zeros_like(acc)
    sums[...] = jnp.zeros_like(sums)

    def prepare(col, stream, slot, slots):
        points = slots * share
        cols = slice(col, col + points)
        pf = part[stream, 0, slot:slot + slots].reshape(points, width)
        pc = part[stream, 1, slot:slot + slots].reshape(points, width)
        hi, lo = split(pf)
        f[cols, 0:width] = hi
        f[cols, width:2 * width] = lo
        hi, lo = hi.T, lo.T
        for n, piece in enumerate((hi, hi, lo, lo)):
            y[n * width:(n + 1) * width, cols] = piece
        norm = jnp.exp2(-scale * jnp.sum(pf * pf, axis=1, keepdims=True))
        hi, lo = split(pc * norm)
        hi, lo = hi.T, lo.T
        hi = jnp.concatenate([hi[rank:], hi[:rank]], axis=0)
        lo = jnp.concatenate([lo[rank:], lo[:rank]], axis=0)
        for n, piece in enumerate((hi, hi, lo, lo)):
            h[n * width:(n + 1) * width, cols] = piece

    def unit(r, points, band=256):
        mine = pl.ds(r * band, band) if isinstance(r, int) else pl.ds(pl.multiple_of(r * band, band), band)
        s = jnp.dot(x[mine, :], y[:, :points], preferred_element_type=F32)
        c = jnp.dot(g[mine, :], h[:, :points], preferred_element_type=F32)
        w = c * jnp.exp2(s)
        total = w[:, :width]
        for k in range(1, points // width):
            total = total + w[:, k * width:(k + 1) * width]
        sums[mine, :] += total
        hi, lo = split(w)
        acc[mine, :] += jnp.dot(hi, f[:points, :], preferred_element_type=F32) + jnp.dot(
            lo, f[:points, :], preferred_element_type=F32
        )

    def bands(first, last, points):
        for r in range(first, last):
            unit(r, points)

    third = 3 * share
    for copy in own:
        copy.wait()
    take_sibling(0)
    prepare(0, 0, 0, 1)
    prepare(share, 1, 0, 1)
    bands(0, 4, 2 * share)
    take_round(1, 0)
    take_round(1, 1)
    for k in (1, 2, 3, 4):
        points = third if k == 1 else 2 * third
        prepare(0, 0, 3 * k - 2, 3)
        if k > 1:
            take_sibling(k - 1)
            prepare(third, 1, 3 * k - 5, 3)
        bands(0, 3, points)
        take_round(k + 1, 0)
        bands(3, 4, points)
        take_round(k + 1, 1)
    take_sibling(4)
    prepare(0, 1, 10, 3)
    bands(0, 4, third)
    take_sibling(5)
    prepare(0, 0, 13, 3)
    prepare(third, 1, 13, 3)

    def reduce_copy(k):
        to = {"blk": blk, "rep": (rep // 2 + 1 + k // 2) % 4 * 2 + (y_lo + 1 + k) % 2}
        return remote(stage.at[k], landed.at[k], red_sent, red_recv, to)

    def finish(n, c):
        r = (rep // 2 + 1 + n) % 4
        unit(r, 768)
        for k in (0, 1):
            lane = pl.ds(pl.multiple_of((r * 2 + (y_lo + 1 + k) % 2) * share, share), share)
            row_sum = jnp.sum(sums[lane, :], axis=1, keepdims=True)
            total = row_sum * feat[lane, :] - (acc[lane, :width] + acc[lane, width:])
            stage[2 * n + k] = total * (-1.0 / width)
        return c

    for n in range(4):
        finish(n, 0)
        for k in (0, 1):
            if 2 * n + k < 7:
                reduce_copy(2 * n + k).start()
    reduced = remote(stage.at[pl.ds(0, 7)], landed, red_sent, red_recv, sibling)
    reduced.wait_recv()
    total = stage[7]
    for k in range(7):
        total = total + landed[k]
    out[...] = total
    reduced.wait_send()
    for fc in (0, 1):
        gathered = part.at[0, fc, pl.ds(1, 15)]
        remote(gathered, gathered, sent, recv.at[0, 0], sibling).wait_send()
    remote(part.at[1], part.at[1], sib_sent, recv.at[0, 0], sibling).wait_send()


def solution(mesh):
    def body(features, factors):
        count, width = features.shape
        share = count // 8
        dma = pltpu.SemaphoreType.DMA
        vmem = pltpu.VMEM
        return pl.pallas_call(
            functools.partial(kernel, count, share, width),
            out_shape=jax.ShapeDtypeStruct((share, width), F32),
            in_specs=[pl.BlockSpec(memory_space=vmem)] * 2,
            out_specs=pl.BlockSpec(memory_space=vmem),
            scratch_shapes=[
                vmem((2, 2, 16, share, width), F32),
                vmem((count, 4 * width), BF16),
                vmem((count, 4 * width), BF16),
                vmem((4 * width, 768), BF16),
                vmem((4 * width, 768), BF16),
                vmem((768, 2 * width), BF16),
                vmem((count, 2 * width), F32),
                vmem((count, width), F32),
                vmem((8, share, width), F32),
                vmem((7, share, width), F32),
                dma((6, 2)),
                dma((6, 2)),
                dma,
                dma,
                dma((2,)),
                dma,
                dma,
            ],
            compiler_params=pltpu.CompilerParams(
                collective_id=0, has_side_effects=True, vmem_limit_bytes=56 * 1024 * 1024
            ),
            name="grads",
        )(features, factors)

    placed = (P("blk", None), P("blk", None))
    return jax.shard_map(
        body, mesh=mesh, in_specs=placed, out_specs=P(("blk", "rep"), None), check_vma=False
    )
```

```python
import functools
import math

import jax
import jax.numpy as jnp
from jax import lax
from jax.experimental import pallas as pl
from jax.experimental.pallas import tpu as pltpu
from jax.sharding import PartitionSpec as P

MESH = pl.DeviceIdType.MESH
F32, BF16 = jnp.float32, jnp.bfloat16

NAMES = ["s0", "s1", "s-1", "o0", "s2", "s-2", "o1", "s3", "s-3", "o2", "o3", "s4", "o-2", "o4", "o-3", "o-1"]
SLOT = {name: i for i, name in enumerate(NAMES)}
SOURCES = [("s0", "s0", "s0"), ("s1", "s-1", "s1"), ("s2", "s-2", "s2"), ("o2", "s-3", "s-2"), ("o3", "o-2", "s-1")]


STEPS = (2, 1, 3, 0)


def split(v):
    hi = v.astype(BF16)
    lo = (v - hi.astype(F32)).astype(BF16)
    return hi, lo


def kernel(count, share, width, feat_in, fac_in, out, feat, fac, part, x, g, y, h, f, acc, sums, stage, landed,
           recv, side_recv, sib_recv, sent, sib_sent, local, loaded, red_sent, red_recv):
    rank = width // 2
    scale = math.log2(math.e) / (2.0 * width)
    blk, rep = lax.axis_index("blk"), lax.axis_index("rep")
    core, zpos, y_hi = blk % 2, (blk // 2) % 8, blk // 16
    y_lo = rep % 2
    down = {"blk": y_hi * 16 + (zpos + 7) % 8 * 2 + core, "rep": rep}
    up = {"blk": y_hi * 16 + (zpos + 1) % 8 * 2 + core, "rep": rep}
    side = {"blk": (1 - y_hi) * 16 + zpos * 2 + core, "rep": rep + 1 - 2 * y_lo}
    sibling = {"blk": blk + 1 - 2 * core, "rep": rep}
    pick = rep // 2 * 2 + (y_lo + y_hi) % 2
    rows = pl.ds(pl.multiple_of(pick * share, share), share)

    barrier = pltpu.get_barrier_semaphore()
    for peer in (down, up, side, sibling):
        pl.semaphore_signal(barrier, inc=1, device_id=peer, device_id_type=MESH)
    for k in range(1, 8):
        pl.semaphore_signal(barrier, inc=1, device_id={"blk": blk, "rep": (rep + k) % 8}, device_id_type=MESH)
    loads = [
        pltpu.make_async_copy((feat_in, fac_in)[fc], (feat, fac)[fc], loaded.at[fc]) for fc in (0, 1)
    ]
    for copy in loads:
        copy.start()
    pl.semaphore_wait(barrier, 11)

    def remote(src, dst, send_sem, recv_sem, to):
        return pltpu.make_async_remote_copy(
            src_ref=src, dst_ref=dst, send_sem=send_sem, recv_sem=recv_sem, device_id=to, device_id_type=MESH
        )

    def send_round(k, fc, names):
        for n, (name, to) in enumerate(zip(SOURCES[k - 1], (down, up, side))):
            if name in names:
                source = part.at[0, fc, SLOT[name]] if name != "s0" else (feat_in, fac_in)[fc].at[rows, :]
                sem = (side_recv if n == 2 else recv).at[k, fc]
                remote(source, part.at[0, fc, 3 * k - 2 + n], sent, sem, to).start()

    def of_round(stream, k, fc):
        return part.at[stream, fc, pl.ds(3 * k - 2, 3)]

    def take_round(k, fc):
        last = NAMES[3 * k]
        along = part.at[0, fc, pl.ds(3 * k - 2, 2)]
        remote(along, along, sent, recv.at[k, fc], sibling).wait_recv()
        if k < 5:
            send_round(k + 1, fc, [name for name in NAMES if name != last])
        across = part.at[0, fc, 3 * k]
        remote(across, across, sent, side_recv.at[k, fc], sibling).wait_recv()
        if k < 5:
            send_round(k + 1, fc, [last])
        remote(of_round(0, k, fc), of_round(1, k, fc), sib_sent, sib_recv.at[k, fc], sibling).start()

    def take_sibling(k):
        for fc in (0, 1):
            buf = of_round(1, k, fc) if k else part.at[1, fc, 0]
            remote(buf, buf, sib_sent, sib_recv.at[k, fc], sibling).wait_recv()

    for fc in (0, 1):
        send_round(1, fc, ["s0"])
    for fc in (0, 1):
        remote((feat_in, fac_in)[fc].at[rows, :], part.at[1, fc, 0], sib_sent, sib_recv.at[0, fc], sibling).start()
    own = [
        pltpu.make_async_copy((feat_in, fac_in)[fc].at[rows, :], part.at[0, fc, 0], local.at[fc]) for fc in (0, 1)
    ]
    for copy in own:
        copy.start()

    for copy in loads:
        copy.wait()
    fo = feat[...]
    norm = jnp.exp2(-scale * jnp.sum(fo * fo, axis=1, keepdims=True))
    for ref, value in ((x, fo * (2.0 * scale)), (g, fac[...] * norm)):
        hi, lo = split(value)
        for k, piece in enumerate((hi, lo, hi, lo)):
            ref[:, k * width:(k + 1) * width] = piece
    acc[...] = jnp.zeros_like(acc)
    sums[...] = jnp.zeros_like(sums)

    def prepare(col, stream, slot, slots):
        points = slots * share
        cols = slice(col, col + points)
        pf = part[stream, 0, slot:slot + slots].reshape(points, width)
        pc = part[stream, 1, slot:slot + slots].reshape(points, width)
        hi, lo = split(pf)
        f[cols, 0:width] = hi
        f[cols, width:2 * width] = lo
        hi, lo = hi.T, lo.T
        for n, piece in enumerate((hi, hi, lo, lo)):
            y[n * width:(n + 1) * width, cols] = piece
        norm = jnp.exp2(-scale * jnp.sum(pf * pf, axis=1, keepdims=True))
        hi, lo = split(pc * norm)
        hi, lo = hi.T, lo.T
        hi = jnp.concatenate([hi[rank:], hi[:rank]], axis=0)
        lo = jnp.concatenate([lo[rank:], lo[:rank]], axis=0)
        for n, piece in enumerate((hi, hi, lo, lo)):
            h[n * width:(n + 1) * width, cols] = piece

    def unit(r, points, band=256):
        mine = pl.ds(r * band, band) if isinstance(r, int) else pl.ds(pl.multiple_of(r * band, band), band)
        s = jnp.dot(x[mine, :], y[:, :points], preferred_element_type=F32)
        c = jnp.dot(g[mine, :], h[:, :points], preferred_element_type=F32)
        w = c * jnp.exp2(s)
        total = w[:, :width]
        for k in range(1, points // width):
            total = total + w[:, k * width:(k + 1) * width]
        sums[mine, :] += total
        hi, lo = split(w)
        acc[mine, :] += jnp.dot(hi, f[:points, :], preferred_element_type=F32) + jnp.dot(
            lo, f[:points, :], preferred_element_type=F32
        )

    def bands(first, last, points):
        for r in range(first, last):
            unit(r, points)

    third = 3 * share
    for copy in own:
        copy.wait()
    take_sibling(0)
    prepare(0, 0, 0, 1)
    prepare(share, 1, 0, 1)
    take_round(1, 0)
    take_round(1, 1)
    for k in (1, 2, 3, 4):
        if k == 1:
            points = 2 * share + third
            prepare(2 * share, 0, 1, 3)
        else:
            points = 2 * third
            prepare(0, 0, 3 * k - 2, 3)
            take_sibling(k - 1)
            prepare(third, 1, 3 * k - 5, 3)
        bands(0, 3, points)
        take_round(k + 1, 0)
        bands(3, 4, points)
        take_round(k + 1, 1)
    take_sibling(4)
    prepare(0, 1, 10, 3)
    prepare(third, 0, 13, 3)
    bands(0, 4, 2 * third)
    take_sibling(5)
    prepare(0, 1, 13, 3)

    def reduce_copy(k):
        to = {"blk": blk, "rep": (rep // 2 + STEPS[k // 2]) % 4 * 2 + (y_lo + 1 + k) % 2}
        return remote(stage.at[k], landed.at[k], red_sent, red_recv, to)

    def finish(k):
        r = (rep // 2 + STEPS[k // 2]) % 4 * 2 + (y_lo + 1 + k) % 2
        lane = pl.ds(pl.multiple_of(r * share, share), share)
        row_sum = jnp.sum(sums[lane, :], axis=1, keepdims=True)
        total = row_sum * feat[lane, :] - (acc[lane, :width] + acc[lane, width:])
        stage[k] = total * (-1.0 / width)

    for n in range(3):
        unit((rep // 2 + STEPS[n]) % 4, third)
        finish(2 * n)
        finish(2 * n + 1)
        reduce_copy(2 * n).start()
        reduce_copy(2 * n + 1).start()
    unit(rep + 1 - 2 * y_lo, third, share)
    finish(6)
    reduce_copy(6).start()
    unit(rep, third, share)
    finish(7)
    reduced = remote(stage.at[pl.ds(0, 7)], landed, red_sent, red_recv, sibling)
    reduced.wait_recv()
    total = stage[7]
    for k in range(7):
        total = total + landed[k]
    out[...] = total
    reduced.wait_send()
    for fc in (0, 1):
        gathered = part.at[0, fc, pl.ds(1, 15)]
        remote(gathered, gathered, sent, recv.at[0, 0], sibling).wait_send()
    remote(part.at[1], part.at[1], sib_sent, recv.at[0, 0], sibling).wait_send()


def solution(mesh):
    def body(features, factors):
        count, width = features.shape
        share = count // 8
        dma = pltpu.SemaphoreType.DMA
        vmem = pltpu.VMEM
        return pl.pallas_call(
            functools.partial(kernel, count, share, width),
            out_shape=jax.ShapeDtypeStruct((share, width), F32),
            in_specs=[pl.BlockSpec(memory_space=pl.ANY)] * 2,
            out_specs=pl.BlockSpec(memory_space=vmem),
            scratch_shapes=[
                vmem((count, width), F32),
                vmem((count, width), F32),
                vmem((2, 2, 16, share, width), F32),
                vmem((count, 4 * width), BF16),
                vmem((count, 4 * width), BF16),
                vmem((4 * width, 768), BF16),
                vmem((4 * width, 768), BF16),
                vmem((768, 2 * width), BF16),
                vmem((count, 2 * width), F32),
                vmem((count, width), F32),
                vmem((8, share, width), F32),
                vmem((7, share, width), F32),
                dma((6, 2)),
                dma((6, 2)),
                dma((6, 2)),
                dma,
                dma,
                dma((2,)),
                dma((2,)),
                dma,
                dma,
            ],
            compiler_params=pltpu.CompilerParams(
                collective_id=0, has_side_effects=True
            ),
            name="grads",
        )(features, factors)

    placed = (P("blk", None), P("blk", None))
    return jax.shard_map(
        body, mesh=mesh, in_specs=placed, out_specs=P(("blk", "rep"), None), check_vma=False
    )
```

```python
import functools
import math

import jax
import jax.numpy as jnp
from jax import lax
from jax.experimental import pallas as pl
from jax.experimental.pallas import tpu as pltpu
from jax.sharding import PartitionSpec as P

MESH = pl.DeviceIdType.MESH
F32, BF16 = jnp.float32, jnp.bfloat16

NAMES = ["s0", "s1", "s-1", "o0", "s2", "s-2", "o1", "s3", "s-3", "o2", "o3", "s4", "o-2", "o4", "o-3", "o-1"]
SLOT = {name: i for i, name in enumerate(NAMES)}
SOURCES = [("s0", "s0", "s0"), ("s1", "s-1", "s1"), ("s2", "s-2", "s2"), ("o2", "s-3", "s-2"), ("o3", "o-2", "s-1")]


STEPS = (2, 1, 3, 0)


def split(v):
    hi = v.astype(BF16)
    lo = (v - hi.astype(F32)).astype(BF16)
    return hi, lo


def kernel(count, share, width, feat_in, fac_in, out, feat, fac, part, x, g, y, h, f, acc, sums, stage, landed,
           recv, side_recv, sib_recv, sent, sib_sent, local, loaded, red_sent, red_recv):
    rank = width // 2
    scale = math.log2(math.e) / (2.0 * width)
    blk, rep = lax.axis_index("blk"), lax.axis_index("rep")
    core, zpos, y_hi = blk % 2, (blk // 2) % 8, blk // 16
    y_lo = rep % 2
    down = {"blk": y_hi * 16 + (zpos + 7) % 8 * 2 + core, "rep": rep}
    up = {"blk": y_hi * 16 + (zpos + 1) % 8 * 2 + core, "rep": rep}
    side = {"blk": (1 - y_hi) * 16 + zpos * 2 + core, "rep": rep + 1 - 2 * y_lo}
    sibling = {"blk": blk + 1 - 2 * core, "rep": rep}
    pick = rep // 2 * 2 + (y_lo + y_hi) % 2
    rows = pl.ds(pl.multiple_of(pick * share, share), share)

    barrier = pltpu.get_barrier_semaphore()
    for peer in (down, up, side, sibling):
        pl.semaphore_signal(barrier, inc=1, device_id=peer, device_id_type=MESH)
    for k in range(1, 8):
        pl.semaphore_signal(barrier, inc=1, device_id={"blk": blk, "rep": (rep + k) % 8}, device_id_type=MESH)
    loads = [
        pltpu.make_async_copy((feat_in, fac_in)[fc], (feat, fac)[fc], loaded.at[fc]) for fc in (0, 1)
    ]
    for copy in loads:
        copy.start()
    pl.semaphore_wait(barrier, 11)

    def remote(src, dst, send_sem, recv_sem, to):
        return pltpu.make_async_remote_copy(
            src_ref=src, dst_ref=dst, send_sem=send_sem, recv_sem=recv_sem, device_id=to, device_id_type=MESH
        )

    half = share // 2

    def send_round(k, fc, cut, names):
        for n, (name, to) in enumerate(zip(SOURCES[k - 1], (down, up, side))):
            if name in names:
                points = pl.ds(cut * half, half)
                if name == "s0":
                    first = pl.multiple_of(pick * share + cut * half, half)
                    source = (feat_in, fac_in)[fc].at[pl.ds(first, half), :]
                else:
                    source = part.at[0, fc, SLOT[name], points]
                sem = (side_recv if n == 2 else recv).at[k, fc, cut]
                remote(source, part.at[0, fc, 3 * k - 2 + n, points], sent, sem, to).start()

    def of_round(stream, k, fc):
        return part.at[stream, fc, pl.ds(3 * k - 2, 3)]

    def take_round(k, fc):
        last = NAMES[3 * k]
        for cut in (0, 1):
            points = pl.ds(cut * half, half)
            along = part.at[0, fc, pl.ds(3 * k - 2, 2), points]
            remote(along, along, sent, recv.at[k, fc, cut], sibling).wait_recv()
            if k < 5:
                send_round(k + 1, fc, cut, [name for name in NAMES if name != last])
            across = part.at[0, fc, 3 * k, points]
            remote(across, across, sent, side_recv.at[k, fc, cut], sibling).wait_recv()
            if k < 5:
                send_round(k + 1, fc, cut, [last])
        remote(of_round(0, k, fc), of_round(1, k, fc), sib_sent, sib_recv.at[k, fc], sibling).start()

    def take_sibling(k):
        for fc in (0, 1):
            buf = of_round(1, k, fc) if k else part.at[1, fc, 0]
            remote(buf, buf, sib_sent, sib_recv.at[k, fc], sibling).wait_recv()

    for fc in (0, 1):
        for cut in (0, 1):
            send_round(1, fc, cut, ["s0"])
    for fc in (0, 1):
        remote((feat_in, fac_in)[fc].at[rows, :], part.at[1, fc, 0], sib_sent, sib_recv.at[0, fc], sibling).start()
    own = [
        pltpu.make_async_copy((feat_in, fac_in)[fc].at[rows, :], part.at[0, fc, 0], local.at[fc]) for fc in (0, 1)
    ]
    for copy in own:
        copy.start()

    for copy in loads:
        copy.wait()
    fo = feat[...]
    norm = jnp.exp2(-scale * jnp.sum(fo * fo, axis=1, keepdims=True))
    for ref, value in ((x, fo * (2.0 * scale)), (g, fac[...] * norm)):
        hi, lo = split(value)
        for k, piece in enumerate((hi, lo, hi, lo)):
            ref[:, k * width:(k + 1) * width] = piece
    acc[...] = jnp.zeros_like(acc)
    sums[...] = jnp.zeros_like(sums)

    def prepare(col, stream, slot, slots):
        points = slots * share
        cols = slice(col, col + points)
        pf = part[stream, 0, slot:slot + slots].reshape(points, width)
        pc = part[stream, 1, slot:slot + slots].reshape(points, width)
        hi, lo = split(pf)
        f[cols, 0:width] = hi
        f[cols, width:2 * width] = lo
        hi, lo = hi.T, lo.T
        for n, piece in enumerate((hi, hi, lo, lo)):
            y[n * width:(n + 1) * width, cols] = piece
        norm = jnp.exp2(-scale * jnp.sum(pf * pf, axis=1, keepdims=True))
        hi, lo = split(pc * norm)
        hi, lo = hi.T, lo.T
        hi = jnp.concatenate([hi[rank:], hi[:rank]], axis=0)
        lo = jnp.concatenate([lo[rank:], lo[:rank]], axis=0)
        for n, piece in enumerate((hi, hi, lo, lo)):
            h[n * width:(n + 1) * width, cols] = piece

    def unit(r, points, band=256):
        mine = pl.ds(r * band, band) if isinstance(r, int) else pl.ds(pl.multiple_of(r * band, band), band)
        s = jnp.dot(x[mine, :], y[:, :points], preferred_element_type=F32)
        c = jnp.dot(g[mine, :], h[:, :points], preferred_element_type=F32)
        w = c * jnp.exp2(s)
        total = w[:, :width]
        for k in range(1, points // width):
            total = total + w[:, k * width:(k + 1) * width]
        sums[mine, :] += total
        hi, lo = split(w)
        acc[mine, :] += jnp.dot(hi, f[:points, :], preferred_element_type=F32) + jnp.dot(
            lo, f[:points, :], preferred_element_type=F32
        )

    def bands(first, last, points):
        for r in range(first, last):
            unit(r, points)

    third = 3 * share
    for copy in own:
        copy.wait()
    take_sibling(0)
    prepare(0, 0, 0, 1)
    prepare(share, 1, 0, 1)
    take_round(1, 0)
    take_round(1, 1)
    for k in (1, 2, 3, 4):
        if k == 1:
            points = 2 * share + third
            prepare(2 * share, 0, 1, 3)
        else:
            points = 2 * third
            prepare(0, 0, 3 * k - 2, 3)
            take_sibling(k - 1)
            prepare(third, 1, 3 * k - 5, 3)
        bands(0, 3, points)
        take_round(k + 1, 0)
        bands(3, 4, points)
        take_round(k + 1, 1)
    take_sibling(4)
    prepare(0, 1, 10, 3)
    prepare(third, 0, 13, 3)
    bands(0, 4, 2 * third)
    take_sibling(5)
    prepare(0, 1, 13, 3)

    def reduce_copy(k):
        to = {"blk": blk, "rep": (rep // 2 + STEPS[k // 2]) % 4 * 2 + (y_lo + 1 + k) % 2}
        return remote(stage.at[k], landed.at[k], red_sent, red_recv, to)

    def finish(k):
        r = (rep // 2 + STEPS[k // 2]) % 4 * 2 + (y_lo + 1 + k) % 2
        lane = pl.ds(pl.multiple_of(r * share, share), share)
        row_sum = jnp.sum(sums[lane, :], axis=1, keepdims=True)
        total = row_sum * feat[lane, :] - (acc[lane, :width] + acc[lane, width:])
        stage[k] = total * (-1.0 / width)

    for n in range(3):
        unit((rep // 2 + STEPS[n]) % 4, third)
        finish(2 * n)
        finish(2 * n + 1)
        reduce_copy(2 * n).start()
        reduce_copy(2 * n + 1).start()
    unit(rep + 1 - 2 * y_lo, third, share)
    finish(6)
    reduce_copy(6).start()
    unit(rep, third, share)
    finish(7)
    reduced = remote(stage.at[pl.ds(0, 7)], landed, red_sent, red_recv, sibling)
    reduced.wait_recv()
    total = stage[7]
    for k in range(7):
        total = total + landed[k]
    out[...] = total
    reduced.wait_send()
    for fc in (0, 1):
        gathered = part.at[0, fc, pl.ds(1, 15)]
        remote(gathered, gathered, sent, recv.at[0, 0, 0], sibling).wait_send()
    remote(part.at[1], part.at[1], sib_sent, recv.at[0, 0, 0], sibling).wait_send()


def solution(mesh):
    def body(features, factors):
        count, width = features.shape
        share = count // 8
        dma = pltpu.SemaphoreType.DMA
        vmem = pltpu.VMEM
        return pl.pallas_call(
            functools.partial(kernel, count, share, width),
            out_shape=jax.ShapeDtypeStruct((share, width), F32),
            in_specs=[pl.BlockSpec(memory_space=pl.ANY)] * 2,
            out_specs=pl.BlockSpec(memory_space=vmem),
            scratch_shapes=[
                vmem((count, width), F32),
                vmem((count, width), F32),
                vmem((2, 2, 16, share, width), F32),
                vmem((count, 4 * width), BF16),
                vmem((count, 4 * width), BF16),
                vmem((4 * width, 768), BF16),
                vmem((4 * width, 768), BF16),
                vmem((768, 2 * width), BF16),
                vmem((count, 2 * width), F32),
                vmem((count, width), F32),
                vmem((8, share, width), F32),
                vmem((7, share, width), F32),
                dma((6, 2, 2)),
                dma((6, 2, 2)),
                dma((6, 2)),
                dma,
                dma,
                dma((2,)),
                dma((2,)),
                dma,
                dma,
            ],
            compiler_params=pltpu.CompilerParams(
                collective_id=0, has_side_effects=True
            ),
            name="grads",
        )(features, factors)

    placed = (P("blk", None), P("blk", None))
    return jax.shard_map(
        body, mesh=mesh, in_specs=placed, out_specs=P(("blk", "rep"), None), check_vma=False
    )
```

```python
import functools
import math

import jax
import jax.numpy as jnp
from jax import lax
from jax.experimental import pallas as pl
from jax.experimental.pallas import tpu as pltpu
from jax.sharding import PartitionSpec as P

MESH = pl.DeviceIdType.MESH
F32, BF16 = jnp.float32, jnp.bfloat16

NAMES = ["s0", "s1", "s-1", "o0", "s2", "s-2", "o1", "s3", "s-3", "o2", "o3", "s4", "o-2", "o4", "o-3", "o-1"]
SLOT = {name: i for i, name in enumerate(NAMES)}
SOURCES = [("s0", "s0", "s0"), ("s1", "s-1", "s1"), ("s2", "s-2", "s2"), ("o2", "s-3", "s-2"), ("o3", "o-2", "s-1")]


STEPS = (2, 1, 3, 0)


def split(v):
    hi = v.astype(BF16)
    lo = (v - hi.astype(F32)).astype(BF16)
    return hi, lo


def kernel(count, share, width, feat_in, fac_in, out, feat, fac, part, x, g, y, h, f, acc, sums, stage, landed,
           recv, side_recv, sib_recv, sent, sib_sent, local, loaded, red_sent, red_recv):
    rank = width // 2
    scale = math.log2(math.e) / (2.0 * width)
    blk, rep = lax.axis_index("blk"), lax.axis_index("rep")
    core, zpos, y_hi = blk % 2, (blk // 2) % 8, blk // 16
    y_lo = rep % 2
    down = {"blk": y_hi * 16 + (zpos + 7) % 8 * 2 + core, "rep": rep}
    up = {"blk": y_hi * 16 + (zpos + 1) % 8 * 2 + core, "rep": rep}
    side = {"blk": (1 - y_hi) * 16 + zpos * 2 + core, "rep": rep + 1 - 2 * y_lo}
    sibling = {"blk": blk + 1 - 2 * core, "rep": rep}
    pick = rep // 2 * 2 + (y_lo + y_hi) % 2
    rows = pl.ds(pl.multiple_of(pick * share, share), share)

    barrier = pltpu.get_barrier_semaphore()
    for peer in (down, up, side, sibling):
        pl.semaphore_signal(barrier, inc=1, device_id=peer, device_id_type=MESH)
    for k in range(1, 8):
        pl.semaphore_signal(barrier, inc=1, device_id={"blk": blk, "rep": (rep + k) % 8}, device_id_type=MESH)
    loads = [
        pltpu.make_async_copy((feat_in, fac_in)[fc], (feat, fac)[fc], loaded.at[fc]) for fc in (0, 1)
    ]
    for copy in loads:
        copy.start()
    pl.semaphore_wait(barrier, 11)

    def remote(src, dst, send_sem, recv_sem, to):
        return pltpu.make_async_remote_copy(
            src_ref=src, dst_ref=dst, send_sem=send_sem, recv_sem=recv_sem, device_id=to, device_id_type=MESH
        )

    half = share // 2

    def send_round(k, fc, cut, names):
        for n, (name, to) in enumerate(zip(SOURCES[k - 1], (down, up, side))):
            if name in names:
                points = pl.ds(cut * half, half)
                if name == "s0":
                    first = pl.multiple_of(pick * share + cut * half, half)
                    source = (feat_in, fac_in)[fc].at[pl.ds(first, half), :]
                else:
                    source = part.at[0, fc, SLOT[name], points]
                sem = (side_recv if n == 2 else recv).at[k, fc, cut]
                remote(source, part.at[0, fc, 3 * k - 2 + n, points], sent, sem, to).start()

    def of_round(stream, k, fc):
        return part.at[stream, fc, pl.ds(3 * k - 2, 3)]

    def take_round(k, fc):
        last = NAMES[3 * k]
        for cut in (0, 1):
            points = pl.ds(cut * half, half)
            along = part.at[0, fc, pl.ds(3 * k - 2, 2), points]
            remote(along, along, sent, recv.at[k, fc, cut], sibling).wait_recv()
            if k < 5:
                send_round(k + 1, fc, cut, [name for name in NAMES if name != last])
        for cut in (0, 1):
            across = part.at[0, fc, 3 * k, pl.ds(cut * half, half)]
            remote(across, across, sent, side_recv.at[k, fc, cut], sibling).wait_recv()
            if k < 5:
                send_round(k + 1, fc, cut, [last])
        remote(of_round(0, k, fc), of_round(1, k, fc), sib_sent, sib_recv.at[k, fc], sibling).start()

    def take_sibling(k):
        for fc in (0, 1):
            buf = of_round(1, k, fc) if k else part.at[1, fc, 0]
            remote(buf, buf, sib_sent, sib_recv.at[k, fc], sibling).wait_recv()

    for fc in (0, 1):
        for cut in (0, 1):
            send_round(1, fc, cut, ["s0"])
    for fc in (0, 1):
        remote((feat_in, fac_in)[fc].at[rows, :], part.at[1, fc, 0], sib_sent, sib_recv.at[0, fc], sibling).start()
    own = [
        pltpu.make_async_copy((feat_in, fac_in)[fc].at[rows, :], part.at[0, fc, 0], local.at[fc]) for fc in (0, 1)
    ]
    for copy in own:
        copy.start()

    for copy in loads:
        copy.wait()
    fo = feat[...]
    norm = jnp.exp2(-scale * jnp.sum(fo * fo, axis=1, keepdims=True))
    for ref, value in ((x, fo * (2.0 * scale)), (g, fac[...] * norm)):
        hi, lo = split(value)
        for k, piece in enumerate((hi, lo, hi, lo)):
            ref[:, k * width:(k + 1) * width] = piece
    acc[...] = jnp.zeros_like(acc)
    sums[...] = jnp.zeros_like(sums)

    def prepare(col, stream, slot, slots):
        points = slots * share
        cols = slice(col, col + points)
        pf = part[stream, 0, slot:slot + slots].reshape(points, width)
        pc = part[stream, 1, slot:slot + slots].reshape(points, width)
        hi, lo = split(pf)
        f[cols, 0:width] = hi
        f[cols, width:2 * width] = lo
        hi, lo = hi.T, lo.T
        for n, piece in enumerate((hi, hi, lo, lo)):
            y[n * width:(n + 1) * width, cols] = piece
        norm = jnp.exp2(-scale * jnp.sum(pf * pf, axis=1, keepdims=True))
        hi, lo = split(pc * norm)
        hi, lo = hi.T, lo.T
        hi = jnp.concatenate([hi[rank:], hi[:rank]], axis=0)
        lo = jnp.concatenate([lo[rank:], lo[:rank]], axis=0)
        for n, piece in enumerate((hi, hi, lo, lo)):
            h[n * width:(n + 1) * width, cols] = piece

    def unit(r, points, band=256):
        mine = pl.ds(r * band, band) if isinstance(r, int) else pl.ds(pl.multiple_of(r * band, band), band)
        s = jnp.dot(x[mine, :], y[:, :points], preferred_element_type=F32)
        c = jnp.dot(g[mine, :], h[:, :points], preferred_element_type=F32)
        w = c * jnp.exp2(s)
        total = w[:, :width]
        for k in range(1, points // width):
            total = total + w[:, k * width:(k + 1) * width]
        sums[mine, :] += total
        hi, lo = split(w)
        acc[mine, :] += jnp.dot(hi, f[:points, :], preferred_element_type=F32) + jnp.dot(
            lo, f[:points, :], preferred_element_type=F32
        )

    def bands(first, last, points):
        for r in range(first, last):
            unit(r, points)

    third = 3 * share
    for copy in own:
        copy.wait()
    take_sibling(0)
    prepare(0, 0, 0, 1)
    prepare(share, 1, 0, 1)
    take_round(1, 0)
    take_round(1, 1)
    for k in (1, 2, 3, 4):
        if k == 1:
            points = 2 * share + third
            prepare(2 * share, 0, 1, 3)
        else:
            points = 2 * third
            prepare(0, 0, 3 * k - 2, 3)
            take_sibling(k - 1)
            prepare(third, 1, 3 * k - 5, 3)
        bands(0, 3, points)
        take_round(k + 1, 0)
        bands(3, 4, points)
        take_round(k + 1, 1)
    take_sibling(4)
    prepare(0, 1, 10, 3)
    prepare(third, 0, 13, 3)
    bands(0, 4, 2 * third)
    take_sibling(5)
    prepare(0, 1, 13, 3)

    def reduce_copy(k):
        to = {"blk": blk, "rep": (rep // 2 + STEPS[k // 2]) % 4 * 2 + (y_lo + 1 + k) % 2}
        return remote(stage.at[k], landed.at[k], red_sent, red_recv, to)

    def finish(k):
        r = (rep // 2 + STEPS[k // 2]) % 4 * 2 + (y_lo + 1 + k) % 2
        lane = pl.ds(pl.multiple_of(r * share, share), share)
        row_sum = jnp.sum(sums[lane, :], axis=1, keepdims=True)
        total = row_sum * feat[lane, :] - (acc[lane, :width] + acc[lane, width:])
        stage[k] = total * (-1.0 / width)

    for n in range(3):
        unit((rep // 2 + STEPS[n]) % 4, third)
        finish(2 * n)
        finish(2 * n + 1)
        reduce_copy(2 * n).start()
        reduce_copy(2 * n + 1).start()
    unit(rep + 1 - 2 * y_lo, third, share)
    finish(6)
    reduce_copy(6).start()
    unit(rep, third, share)
    finish(7)
    reduced = remote(stage.at[pl.ds(0, 7)], landed, red_sent, red_recv, sibling)
    reduced.wait_recv()
    total = stage[7]
    for k in range(7):
        total = total + landed[k]
    out[...] = total
    reduced.wait_send()
    for fc in (0, 1):
        gathered = part.at[0, fc, pl.ds(1, 15)]
        remote(gathered, gathered, sent, recv.at[0, 0, 0], sibling).wait_send()
    remote(part.at[1], part.at[1], sib_sent, recv.at[0, 0, 0], sibling).wait_send()


def solution(mesh):
    def body(features, factors):
        count, width = features.shape
        share = count // 8
        dma = pltpu.SemaphoreType.DMA
        vmem = pltpu.VMEM
        return pl.pallas_call(
            functools.partial(kernel, count, share, width),
            out_shape=jax.ShapeDtypeStruct((share, width), F32),
            in_specs=[pl.BlockSpec(memory_space=pl.ANY)] * 2,
            out_specs=pl.BlockSpec(memory_space=vmem),
            scratch_shapes=[
                vmem((count, width), F32),
                vmem((count, width), F32),
                vmem((2, 2, 16, share, width), F32),
                vmem((count, 4 * width), BF16),
                vmem((count, 4 * width), BF16),
                vmem((4 * width, 768), BF16),
                vmem((4 * width, 768), BF16),
                vmem((768, 2 * width), BF16),
                vmem((count, 2 * width), F32),
                vmem((count, width), F32),
                vmem((8, share, width), F32),
                vmem((7, share, width), F32),
                dma((6, 2, 2)),
                dma((6, 2, 2)),
                dma((6, 2)),
                dma,
                dma,
                dma((2,)),
                dma((2,)),
                dma,
                dma,
            ],
            compiler_params=pltpu.CompilerParams(
                collective_id=0, has_side_effects=True
            ),
            name="grads",
        )(features, factors)

    placed = (P("blk", None), P("blk", None))
    return jax.shard_map(
        body, mesh=mesh, in_specs=placed, out_specs=P(("blk", "rep"), None), check_vma=False
    )
```
